32 devices in a mesh: ctx: 8 (over z, x), head: 4 (over y, core).
Axes of the slice: x: 2, y: 2, z: 4, core: 2. Of those that a mesh axis runs over, the one named last changes fastest.
Arguments:
- signal: bfloat16 [6144, 5120], P(('ctx', 'head')), may hold values from -0.125 to 0.125
- cotangent: bfloat16 [6144, 5120], P(('ctx', 'head')), may hold values from -0.125 to 0.125
- input_map: bfloat16 [6144, 128], P('ctx'), may hold values from -1.75 to 1.75
- output_map: bfloat16 [6144, 128], P('ctx'), may hold values from -1.75 to 1.75
- log_decay: float32 [6144, 80], P('ctx', 'head'), may hold values from -1 to 0, as said below
- skip_gain: float32 [80], P('head'), may hold values from 0.5 to 2
Outputs:
- scan_out: bfloat16 [6144, 5120], P(('ctx', 'head'))
- grad_signal: bfloat16 [6144, 5120], P(('ctx', 'head'))
- grad_input_map: float32 [6144, 128], P('ctx')
- grad_output_map: float32 [6144, 128], P('ctx')
- grad_decay: float32 [6144, 80], P('ctx', 'head')
The draws below stay inside these ranges and needn't reach their ends.
Inputs may be any that keep to these rules, and one draw needn't show every extreme that they name: `log_decay`: every entry is negative.
All inputs are finite; a program needn't handle non-finite values.
Results may differ from the reference program's by a relative error of at most 0.0027.
Values may be sent and summed in bfloat16 or wider, within the bound.
A program may use at most 192 MiB of HBM per device.

```python
import math
import jax
import jax.numpy as jnp
from jax import lax

H = 80
STATE = 128
GROUP_POSITIONS = 256
INNER = 5120
CTX_LEN = 768
SEQUENCE_TOKENS = 6144
N_CTX = 8


def draw_log_decay(key, part):
    random_keys = jax.random.split(key, 7)
    kinds = jax.random.randint(random_keys[0], (H,), 0, 4)
    fast_heads = kinds >= 2
    slow_rate = jnp.exp(jax.random.uniform(random_keys[1], (H,), minval=math.log(0.0001), maxval=math.log(0.001)))
    fast_rate = jnp.exp(jax.random.uniform(random_keys[2], (H,), minval=math.log(1.0 / 50.0), maxval=math.log(1.0 / 30.0)))
    baseline_rate = jnp.where(fast_heads, fast_rate, slow_rate)
    block_count = SEQUENCE_TOKENS // CTX_LEN
    block_multiplier = jnp.exp(jax.random.uniform(random_keys[3], (block_count, H), minval=math.log(0.6), maxval=math.log(1.4)))
    block_multiplier = jnp.repeat(block_multiplier, CTX_LEN, axis=0)
    surface_jitter = jax.random.uniform(random_keys[4], (SEQUENCE_TOKENS, H), minval=0.5, maxval=1.5)
    spike_count = max(SEQUENCE_TOKENS // (4 * GROUP_POSITIONS), 3)
    token_positions = jax.random.randint(random_keys[5], (spike_count,), 0, SEQUENCE_TOKENS)
    loss_values = jax.random.uniform(random_keys[6], (spike_count,), minval=0.2, maxval=0.35)
    device_places = jnp.arange(SEQUENCE_TOKENS)
    spike_events = jnp.sum(jnp.where(device_places[:, None] == token_positions[None, :], jnp.log1p(-loss_values)[None, :], 0.0), axis=1)
    value_rows = -baseline_rate[None, :] * block_multiplier * surface_jitter + spike_events[:, None]
    return value_rows.astype(jnp.float32)


def levels(own_key, shape, cuts, low, top_value):
    level, own = 1.0, jax.random.fold_in(own_key, 6)
    for position, shards_of in cuts:
        heights = jnp.exp(jax.random.uniform(jax.random.fold_in(own, position), (shards_of,), jnp.float32, low / len(cuts), top_value / len(cuts)))
        level = level * jnp.repeat(heights, shape[position] // shards_of).reshape([-1 if axis == position else 1 for axis in range(len(shape))])
    return level


def scatter_about(stream_key, dims, scale, limit, cuts=(), held_as=jnp.bfloat16):
    values = jax.random.normal(stream_key, dims, jnp.float32) * scale
    if len(cuts) > 0:
        values = levels(stream_key, dims, cuts, -0.22, 0.18) * values
    return jnp.clip(values, min=-limit, max=limit).astype(held_as)


def setup_inputs(seed: int = 0) -> dict:
    keys = jax.random.split(jax.random.key(seed), 7)
    signal = scatter_about(keys[0], (SEQUENCE_TOKENS, INNER), 0.02, 0.125, ((0, 32),))
    cotangent = scatter_about(keys[1], (SEQUENCE_TOKENS, INNER), 0.02, 0.125, ((0, 32),))
    input_map = scatter_about(keys[2], (SEQUENCE_TOKENS, STATE), 0.3, 1.75, ((0, 8),))
    output_map = scatter_about(keys[3], (SEQUENCE_TOKENS, STATE), 0.3, 1.75, ((0, 8),))
    log_decay = draw_log_decay(jax.random.fold_in(keys[6], 71), 0)
    skip_gain = jnp.clip(0.5 + 1.5 * jax.random.uniform(keys[5], (H,), jnp.float32) ** levels(keys[5], (H,), ((0, 4),), -0.2, 0.2), 0.5, 2.0)
    return {"signal": signal, "cotangent": cotangent, "input_map": input_map, "output_map": output_map, "log_decay": log_decay, "skip_gain": skip_gain}


exact_mode = lax.Precision.HIGHEST

def decay_tables(log_decay, group_len):
    length, head_count = log_decay.shape
    groups = length // group_len
    inside = jnp.cumsum(log_decay.reshape(groups, group_len, head_count), axis=1)
    totals = inside[:, -1, :]
    across = jnp.cumsum(totals, axis=0)
    return (inside, totals, across, across - totals)

def local_block(signal_full, inputs_full, outputs_full, log_decay, skip_gain, group_len):
    length, head_count = log_decay.shape
    groups = length // group_len
    inside, totals, across, before = decay_tables(log_decay, group_len)
    signal_blocks = signal_full.reshape(groups, group_len, head_count, -1)
    inputs_blocks = inputs_full.reshape(groups, group_len, -1)
    outputs_blocks = outputs_full.reshape(groups, group_len, -1)
    scores = jnp.einsum('cin,cjn->cij', outputs_blocks, inputs_blocks, precision=exact_mode)
    by_head = jnp.swapaxes(inside, 1, 2)
    causal = lax.broadcasted_iota(jnp.int32, (group_len, group_len), 0) >= lax.broadcasted_iota(jnp.int32, (group_len, group_len), 1)
    differences = jnp.where(causal, by_head[:, :, :, None] - by_head[:, :, None, :], 0.0)
    decays = jnp.where(causal, jnp.exp(differences), 0.0)
    weights = lax.optimization_barrier((scores[:, None, :, :] * decays).astype(jnp.bfloat16)).astype(jnp.float32)
    within = jnp.einsum('chij,cjhp->cihp', weights, signal_blocks, precision=exact_mode)
    to_end = jnp.exp(totals[:, None, :] - inside)
    states = jnp.einsum('cqhp,cqn->chpn', signal_blocks * to_end[..., None], inputs_blocks, precision=exact_mode)
    later_mask = lax.broadcasted_iota(jnp.int32, (groups, groups), 0) > lax.broadcasted_iota(jnp.int32, (groups, groups), 1)
    spans_log = jnp.where(later_mask[:, :, None], before[:, None, :] - across[None, :, :], 0.0)
    carry_weights = jnp.where(later_mask[:, :, None], jnp.exp(spans_log), 0.0)
    entering = jnp.einsum('kch,chpn->khpn', carry_weights, states, precision=exact_mode)
    carried_in = jnp.einsum('cqn,chpn->cqhp', outputs_blocks, entering, precision=exact_mode) * jnp.exp(inside)[..., None]
    combined = within + carried_in + skip_gain[None, None, :, None] * signal_blocks
    closing = jnp.einsum('ch,chpn->hpn', jnp.exp(across[-1][None, :] - across), states, precision=exact_mode)
    return (combined.reshape(length, -1), closing)

def carried_part(outputs_full, log_decay, incoming):
    length, head_count = log_decay.shape
    running = jnp.cumsum(log_decay, axis=0)
    portion = jnp.einsum('tn,hpn->thp', outputs_full, incoming, precision=exact_mode) * jnp.exp(running)[..., None]
    return (portion.reshape(length, -1), jnp.exp(running[-1])[:, None, None] * incoming)

def backward_seed(tangent_full, outputs_full, log_decay):
    length, head_count = log_decay.shape
    running = jnp.cumsum(log_decay, axis=0)
    weighted = tangent_full.reshape(length, head_count, -1) * jnp.exp(running)[..., None]
    return jnp.einsum('thp,tn->hpn', weighted, outputs_full, precision=exact_mode)

def reference(signal, cotangent, input_map, output_map, log_decay, skip_gain):
    blocks = N_CTX
    block_len = SEQUENCE_TOKENS // N_CTX
    signal_all = signal.astype(jnp.float32).reshape(blocks, block_len, -1)
    tangent_all = cotangent.astype(jnp.float32).reshape(blocks, block_len, -1)
    inputs_all = input_map.astype(jnp.float32).reshape(blocks, block_len, -1)
    outputs_all = output_map.astype(jnp.float32).reshape(blocks, block_len, -1)
    decay_all = log_decay.reshape(blocks, block_len, -1)

    def first_pass(pieces):
        signal_full, tangent_full, inputs_full, outputs_full, decay_full = pieces
        closing = local_block(signal_full, inputs_full, outputs_full, decay_full, skip_gain, GROUP_POSITIONS)[1]
        retained = jnp.exp(jnp.cumsum(decay_full, axis=0)[-1])
        return (closing, retained, backward_seed(tangent_full, outputs_full, decay_full))
    closings, retains, seeds = lax.map(first_pass, (signal_all, tangent_all, inputs_all, outputs_all, decay_all))

    def chain_step(carry, pieces):
        retained, addition = pieces
        return (retained[:, None, None] * carry + addition, carry)
    zero_state = jnp.zeros_like(closings[0])
    final_fwd, enterings = lax.scan(chain_step, zero_state, (retains, closings))
    final_bwd, leavings = lax.scan(chain_step, zero_state, (retains, seeds), reverse=True)

    def second_pass(pieces):
        signal_full, tangent_full, inputs_full, outputs_full, decay_full, entering, leaving = pieces

        def own_part(signal_part, inputs_part, outputs_part, decay_part):
            return local_block(signal_part, inputs_part, outputs_part, decay_part, skip_gain, GROUP_POSITIONS)
        (own_out, own_state), own_pull = jax.vjp(own_part, signal_full, inputs_full, outputs_full, decay_full)
        (carried, passed), carry_pull = jax.vjp(carried_part, outputs_full, decay_full, entering)
        combined = (own_out + carried).astype(jnp.bfloat16)
        grad_sig, grad_in, grad_out_a, grad_decay_a = own_pull((tangent_full, leaving))
        grad_out_b, grad_decay_b, unused = carry_pull((tangent_full, leaving))
        return (combined, grad_sig.astype(jnp.bfloat16), grad_in, grad_out_a + grad_out_b, grad_decay_a + grad_decay_b)
    results = lax.map(second_pass, (signal_all, tangent_all, inputs_all, outputs_all, decay_all, enterings, leavings))
    scan_out = results[0].reshape(SEQUENCE_TOKENS, -1)
    grad_signal = results[1].reshape(SEQUENCE_TOKENS, -1)
    grad_input_map = results[2].reshape(SEQUENCE_TOKENS, -1)
    grad_output_map = results[3].reshape(SEQUENCE_TOKENS, -1)
    grad_decay = results[4].reshape(SEQUENCE_TOKENS, -1)
    return (scan_out, grad_signal, grad_input_map, grad_output_map, grad_decay)
```

```python
import jax
import jax.numpy as jnp
from jax import lax
from jax.experimental import pallas as pl
from jax.experimental.pallas import tpu as pltpu
from jax.sharding import PartitionSpec as P

F32, BF16, F16 = jnp.float32, jnp.bfloat16, jnp.float16
TINY = 1e-30
STEP_HEADS = 8


def split(value):
    high = value.astype(BF16)
    return high, (value - high.astype(F32)).astype(BF16)


def dot(a, b, ca, cb):
    return lax.dot_general(a, b, (((ca,), (cb,)), ((), ())), preferred_element_type=F32)


def column(table, lanes, head):
    return jnp.sum(jnp.where(lanes == head, table, 0.0), axis=1, keepdims=True)


def states_kernel(x_ref, dy_ref, cum_ref, b_ref, c_ref, s_ref, r_ref, *, per, width):
    step = pl.program_id(0)
    cum = cum_ref[...]
    length = cum.shape[0]
    lanes = lax.broadcasted_iota(jnp.int32, cum.shape, 1)
    half = lax.broadcasted_iota(jnp.int32, (length, 2 * width), 1) < width
    into, outof = b_ref[...], c_ref[...]
    for pair in range(per // 2):
        first = column(cum, lanes, step * per + 2 * pair)
        second = column(cum, lanes, step * per + 2 * pair + 1)
        both = jnp.where(half, first, second)
        total = both[length - 1 : length, :]
        at = slice(pair * 2 * width, (pair + 1) * 2 * width)
        xs = split(x_ref[:, at].astype(F32) * jnp.exp(total - both))
        ds = split(dy_ref[:, at].astype(F32) * jnp.exp(both))
        s_ref[at, :] = dot(xs[0], into, 0, 0) + dot(xs[1], into, 0, 0)
        r_ref[at, :] = dot(ds[0], outof, 0, 0) + dot(ds[1], outof, 0, 0)


def within_kernel(
    x_ref, dy_ref, cum_ref, cumt_ref, b_ref, c_ref, gain_ref,
    y_ref, dx_ref, dsc_ref, rows_ref, cols_ref, scores_ref, *, per, width,
):
    step = pl.program_id(0)

    @pl.when(step == 0)
    def _():
        scores_ref[...] = dot(c_ref[...], b_ref[...], 1, 1)
        dsc_ref[...] = jnp.zeros_like(dsc_ref)
        rows_ref[...] = jnp.zeros_like(rows_ref)

    cum = cum_ref[...]
    length = cum.shape[0]
    lanes = lax.broadcasted_iota(jnp.int32, cum.shape, 1)
    causal = lax.broadcasted_iota(jnp.int32, (length, length), 0) >= lax.broadcasted_iota(
        jnp.int32, (length, length), 1
    )
    for pair in range(per // 2):
        outs, grads = [], []
        for h in (2 * pair, 2 * pair + 1):
            head = step * per + h
            at = slice(h * width, (h + 1) * width)
            x, dy = x_ref[:, at], dy_ref[:, at]
            col = column(cum, lanes, head)
            row = cumt_ref[h : h + 1, :]
            decay = jnp.exp(jnp.where(causal, col - row, -1e30))
            weights = scores_ref[...] * decay
            narrow = weights.astype(BF16)
            outs.append(dot(narrow, x, 1, 0))
            grads.append(dot(narrow, dy, 0, 0))
            dw = dot(dy, x, 1, 1).astype(BF16).astype(F32)
            dsc_ref[...] += dw * decay
            pull = dw * weights
            rows_ref[...] += jnp.where(lanes == head, jnp.sum(pull, axis=1, keepdims=True), 0.0)
            cols_ref[h : h + 1, :] = jnp.sum(pull, axis=0, keepdims=True)
        at = slice(pair * 2 * width, (pair + 1) * 2 * width)
        gain = gain_ref[:, at]
        y_ref[:, at] = jnp.concatenate(outs, axis=1) + gain * x_ref[:, at].astype(F32)
        dx_ref[:, at] = jnp.concatenate(grads, axis=1) + gain * dy_ref[:, at].astype(F32)


def carried_kernel(
    x_ref, dy_ref, y_ref, dx_ref, e_ref, l_ref, cum_ref, b_ref, c_ref, dsc_ref, net_ref,
    out_ref, grad_ref, db_ref, dc_ref, dla_ref, q_ref, r_ref, el_ref, *, per, width,
):
    step = pl.program_id(0)

    @pl.when(step == 0)
    def _():
        q_ref[...] = net_ref[...]
        r_ref[...] = jnp.zeros_like(r_ref)
        el_ref[...] = jnp.zeros_like(el_ref)
        high, low = split(dsc_ref[...])
        db_ref[...] = dot(high, c_ref[...], 0, 0) + dot(low, c_ref[...], 0, 0)
        dc_ref[...] = dot(high, b_ref[...], 1, 0) + dot(low, b_ref[...], 1, 0)

    cum = cum_ref[...]
    length = cum.shape[0]
    lanes = lax.broadcasted_iota(jnp.int32, cum.shape, 1)
    lane_row = lanes[0:1, :]
    half = lax.broadcasted_iota(jnp.int32, (length, 2 * width), 1) < width
    into, outof = b_ref[...], c_ref[...]
    add_b, add_c = jnp.zeros_like(db_ref), jnp.zeros_like(dc_ref)
    add_q, add_r, add_el = jnp.zeros_like(q_ref), jnp.zeros_like(r_ref), jnp.zeros_like(el_ref)
    for pair in range(per // 2):
        head = step * per + 2 * pair
        both = jnp.where(half, column(cum, lanes, head), column(cum, lanes, head + 1))
        total = both[length - 1 : length, :]
        grow, tail = jnp.exp(both), jnp.exp(total - both)
        at = slice(pair * 2 * width, (pair + 1) * 2 * width)
        x, dy = x_ref[:, at].astype(F32), dy_ref[:, at].astype(F32)
        entering, leaving = e_ref[at, :], l_ref[at, :]
        eh, el = split(entering)
        lh, ll = split(leaving)
        carried = (dot(outof, eh, 1, 1) + dot(outof, el, 1, 1)) * grow
        pulled = (dot(into, lh, 1, 1) + dot(into, ll, 1, 1)) * tail
        out_ref[:, at] = (y_ref[:, at] + carried).astype(BF16)
        grad_ref[:, at] = (dx_ref[:, at] + pulled).astype(BF16)
        zh, zl = split(dy * grow)
        add_c += dot(zh, eh, 1, 0) + dot(zl, eh, 1, 0) + dot(zh, el, 1, 0)
        uh, ul = split(x * tail)
        add_b += dot(uh, lh, 1, 0) + dot(ul, lh, 1, 0) + dot(uh, ll, 1, 0)
        q, r, prod = dy * carried, x * pulled, entering * leaving
        for h in (0, 1):
            mine = half if h == 0 else jnp.logical_not(half)
            mark = lanes == head + h
            add_q += jnp.where(mark, jnp.sum(jnp.where(mine, q, 0.0), axis=1, keepdims=True), 0.0)
            add_r += jnp.where(mark, jnp.sum(jnp.where(mine, r, 0.0), axis=1, keepdims=True), 0.0)
            part = jnp.sum(prod[h * width : (h + 1) * width, :], axis=0, keepdims=True)
            add_el += jnp.where(lane_row == head + h, jnp.sum(part, axis=1, keepdims=True), 0.0)
    db_ref[...] += add_b
    dc_ref[...] += add_c
    q_ref[...] += add_q
    r_ref[...] += add_r
    el_ref[...] += add_el

    @pl.when(step == pl.num_programs(0) - 1)
    def _():
        i = lax.broadcasted_iota(jnp.int32, (length, length), 0)
        j = lax.broadcasted_iota(jnp.int32, (length, length), 1)
        after, before = (j >= i).astype(BF16), (j < i).astype(BF16)
        qh, ql = split(q_ref[...])
        rh, rl = split(r_ref[...])
        dla_ref[...] = (
            dot(after, qh, 1, 0) + dot(after, ql, 1, 0) + dot(before, rh, 1, 0) + dot(before, rl, 1, 0)
            + jnp.exp(cum[length - 1 : length, :]) * el_ref[...]
        )


def later_sum(logs, own=None):
    count = logs.shape[0]
    i = lax.broadcasted_iota(jnp.int32, (count, count), 0)
    j = lax.broadcasted_iota(jnp.int32, (count, count), 1)
    keep = (j > i) if own is None else (j > i) & (j < own)
    return jnp.sum(jnp.where(keep[:, :, None], logs[None], 0.0), axis=1)


def group_factors(meta, ctx, blocks, members):
    total, peak = meta[:, :, 0], meta[:, :, 1]
    to_end = jax.vmap(later_sum)(total)
    bound = jnp.sum(jnp.exp(to_end) * peak, axis=1)
    sums = jnp.sum(total, axis=1)
    earlier = lax.broadcasted_iota(jnp.int32, (blocks, 1), 0) < ctx
    reach = jnp.where(earlier, jnp.exp(later_sum(sums, ctx)), 0.0) * bound
    own_total = lax.dynamic_index_in_dim(total, ctx, 0, keepdims=False)
    own_peak = lax.dynamic_index_in_dim(peak, ctx, 0, keepdims=False)
    own_to_end = lax.dynamic_index_in_dim(to_end, ctx, 0, keepdims=False)
    limit = [jnp.sum(reach, axis=0)]
    for s in range(members - 1):
        limit.append(jnp.exp(own_total[s]) * limit[-1] + own_peak[s])
    return dict(
        peak=own_peak, factor=jnp.exp(own_to_end), keep=jnp.exp(own_total),
        bound=lax.dynamic_index_in_dim(bound, ctx, 0, keepdims=False),
        reach=reach, limit=jnp.stack(limit),
    )


def shards(signal, cotangent, input_map, output_map, log_decay, skip_gain):
    members, blocks = lax.axis_size("head"), lax.axis_size("ctx")
    member, ctx = lax.axis_index("head"), lax.axis_index("ctx")
    length, channels = signal.shape
    own_heads = log_decay.shape[1]
    heads = own_heads * members
    width = channels // heads
    state = input_map.shape[1]
    per = STEP_HEADS
    steps = heads // per
    lane_block = per * width

    decay = lax.all_to_all(log_decay, "head", split_axis=0, concat_axis=1, tiled=True)
    gains = lax.all_gather(skip_gain, "head", tiled=True)
    into = lax.dynamic_slice_in_dim(input_map, member * length, length, 0)
    outof = lax.dynamic_slice_in_dim(output_map, member * length, length, 0)
    lower = (
        lax.broadcasted_iota(jnp.int32, (length, length), 0)
        >= lax.broadcasted_iota(jnp.int32, (length, length), 1)
    ).astype(F32)
    cum = jnp.dot(lower, decay, precision=lax.Precision.HIGHEST)
    cum_t = cum.T
    gain_row = jnp.repeat(gains, width)[None, :]

    wide = pl.BlockSpec((length, lane_block), lambda k: (0, k))
    tall = pl.BlockSpec((lane_block, state), lambda k: (k, 0))

    def whole(*shape):
        return pl.BlockSpec(shape, lambda k: (0, 0))

    def call(body, name, in_specs, out_specs, out_shape, scratch=(), flops=0):
        return pl.pallas_call(
            lambda *refs: body(*refs, per=per, width=width),
            grid=(steps,), in_specs=in_specs, out_specs=out_specs, out_shape=out_shape,
            scratch_shapes=scratch, name=name,
            cost_estimate=pl.CostEstimate(flops=flops, transcendentals=0, bytes_accessed=16 * length * channels),
        )

    sd = jax.ShapeDtypeStruct
    maps = [whole(length, state)] * 2
    own_state, own_seed = call(
        states_kernel, "states", [wide, wide, whole(length, heads)] + maps, [tall, tall],
        [sd((channels, state), F32)] * 2, flops=8 * length * channels * state,
    )(signal, cotangent, cum, into, outof)

    def peak_of(value):
        return jnp.maximum(jnp.max(jnp.abs(value.reshape(heads, -1)), axis=1), TINY)

    own_meta = jnp.stack([cum[-1], peak_of(own_state), peak_of(own_seed)])
    meta = lax.all_gather(own_meta, ("ctx", "head")).reshape(blocks, members, 3, heads)

    def scaled(value, scale):
        return value.reshape(heads, width, state) / scale[:, None, None]

    packed = jnp.concatenate(
        [scaled(own_state, own_meta[1]), scaled(own_seed, own_meta[2])], axis=2
    ).astype(F16)
    arrived = lax.all_to_all(packed, "head", split_axis=0, concat_axis=0, tiled=True)
    arrived = arrived.reshape(members, own_heads, width, 2 * state).astype(F32)

    y_local, dx_local, dscores, rows, cols = call(
        within_kernel, "within",
        [wide, wide, whole(length, heads), pl.BlockSpec((per, length), lambda k: (k, 0))] + maps
        + [pl.BlockSpec((1, lane_block), lambda k: (0, k))],
        [wide, wide, whole(length, length), whole(length, heads),
         pl.BlockSpec((per, length), lambda k: (k, 0))],
        [sd((length, channels), F32)] * 2
        + [sd((length, length), F32), sd((length, heads), F32), sd((heads, length), F32)],
        scratch=[pltpu.VMEM((length, length), F32)], flops=24 * length * length * channels,
    )(signal, cotangent, cum, cum_t, into, outof, gain_row)

    forward = group_factors(meta[:, :, (0, 1)], ctx, blocks, members)
    back = group_factors(meta[::-1, ::-1, (0, 2)], blocks - 1 - ctx, blocks, members)

    def mine(table):
        return lax.dynamic_slice_in_dim(table, member * own_heads, own_heads, table.ndim - 1)[
            ..., None, None
        ]

    fwd = {k: mine(v) for k, v in forward.items()}
    bwd = {k: mine(v) for k, v in back.items()}
    parts_f = arrived[..., :state] * fwd["peak"]
    parts_b = arrived[::-1, ..., state:] * bwd["peak"]
    group_f = jnp.sum(parts_f * fwd["factor"], axis=0) / jnp.maximum(fwd["bound"], TINY)
    group_b = jnp.sum(parts_b * bwd["factor"], axis=0) / jnp.maximum(bwd["bound"], TINY)
    sums = lax.all_gather(jnp.concatenate([group_f, group_b], axis=2).astype(F16), "ctx").astype(F32)
    entering = jnp.sum(sums[..., :state] * fwd["reach"], axis=0)
    leaving = jnp.sum(sums[..., state:] * bwd["reach"][::-1], axis=0)
    list_f, list_b = [entering], [leaving]
    for s in range(members - 1):
        list_f.append(fwd["keep"][s] * list_f[-1] + parts_f[s])
        list_b.append(bwd["keep"][s] * list_b[-1] + parts_b[s])
    send_f = jnp.stack(list_f) / jnp.maximum(fwd["limit"], TINY)
    send_b = (jnp.stack(list_b) / jnp.maximum(bwd["limit"], TINY))[::-1]
    send = jnp.concatenate([send_f, send_b], axis=3).astype(F16)
    back_home = lax.all_to_all(
        send.reshape(heads, width, 2 * state), "head", split_axis=0, concat_axis=0, tiled=True
    ).astype(F32)
    limit_f = lax.dynamic_index_in_dim(forward["limit"], member, 0, keepdims=False)
    limit_b = lax.dynamic_index_in_dim(back["limit"], members - 1 - member, 0, keepdims=False)
    e_all = (back_home[..., :state] * limit_f[:, None, None]).reshape(channels, state)
    l_all = (back_home[..., state:] * limit_b[:, None, None]).reshape(channels, state)

    scan_out, grad_signal, grad_in, grad_out, grad_decay = call(
        carried_kernel, "carried",
        [wide, wide, wide, wide, tall, tall, whole(length, heads)] + maps
        + [whole(length, length), whole(length, heads)],
        [wide, wide, whole(length, state), whole(length, state), whole(length, heads)],
        [sd((length, channels), BF16)] * 2 + [sd((length, state), F32)] * 2 + [sd((length, heads), F32)],
        scratch=[pltpu.VMEM((length, heads), F32)] * 2 + [pltpu.VMEM((1, heads), F32)],
        flops=20 * length * channels * state,
    )(signal, cotangent, y_local, dx_local, e_all, l_all, cum, into, outof, dscores, rows - cols.T)

    maps_out = lax.all_gather(jnp.concatenate([grad_in, grad_out], axis=1), "head", tiled=True)
    grad_decay = lax.all_to_all(grad_decay, "head", split_axis=1, concat_axis=0, tiled=True)
    return (scan_out, grad_signal, maps_out[:, :state], maps_out[:, state:], grad_decay)


def solution(mesh):
    return jax.shard_map(
        shards,
        mesh=mesh,
        in_specs=(
            P(("ctx", "head"), None),
            P(("ctx", "head"), None),
            P("ctx", None),
            P("ctx", None),
            P("ctx", "head"),
            P("head"),
        ),
        out_specs=(
            P(("ctx", "head"), None),
            P(("ctx", "head"), None),
            P("ctx", None),
            P("ctx", None),
            P("ctx", "head"),
        ),
        check_vma=False,
    )
```

```python
import jax
import jax.numpy as jnp
from jax import lax
from jax.experimental import pallas as pl
from jax.experimental.pallas import tpu as pltpu
from jax.sharding import PartitionSpec as P

F32, BF16, F16 = jnp.float32, jnp.bfloat16, jnp.float16
TINY = 1e-30
STEP_HEADS = 8
TAIL_ROWS = 16


def split(value):
    high = value.astype(BF16)
    return high, (value - high.astype(F32)).astype(BF16)


def dot(a, b, ca, cb):
    return lax.dot_general(a, b, (((ca,), (cb,)), ((), ())), preferred_element_type=F32)


def column(table, lanes, head):
    return jnp.sum(jnp.where(lanes == head, table, 0.0), axis=1, keepdims=True)


def states_kernel(x_ref, dy_ref, cum_ref, b_ref, c_ref, s_ref, r_ref, *, per, width):
    step = pl.program_id(0)
    cum = cum_ref[...]
    length = cum.shape[0]
    lanes = lax.broadcasted_iota(jnp.int32, cum.shape, 1)
    half = lax.broadcasted_iota(jnp.int32, (length, 2 * width), 1) < width
    into, outof = b_ref[...], c_ref[...]
    for pair in range(per // 2):
        first = column(cum, lanes, step * per + 2 * pair)
        second = column(cum, lanes, step * per + 2 * pair + 1)
        both = jnp.where(half, first, second)
        total = both[length - 1 : length, :]
        at = slice(pair * 2 * width, (pair + 1) * 2 * width)
        xs = split(x_ref[:, at].astype(F32) * jnp.exp(total - both))
        ds = split(dy_ref[:, at].astype(F32) * jnp.exp(both))
        s_ref[at, :] = dot(xs[0], into, 0, 0) + dot(xs[1], into, 0, 0)
        r_ref[at, :] = dot(ds[0], outof, 0, 0) + dot(ds[1], outof, 0, 0)


def within_kernel(
    x_ref, dy_ref, cum_ref, cumt_ref, b_ref, c_ref, gain_ref,
    y_ref, dx_ref, dsc_ref, rows_ref, cols_ref, scores_ref, *, per, width,
):
    step = pl.program_id(0)

    @pl.when(step == 0)
    def _():
        scores_ref[...] = dot(c_ref[...], b_ref[...], 1, 1)
        dsc_ref[...] = jnp.zeros_like(dsc_ref)
        rows_ref[...] = jnp.zeros_like(rows_ref)

    cum = cum_ref[...]
    length = cum.shape[0]
    lanes = lax.broadcasted_iota(jnp.int32, cum.shape, 1)
    causal = lax.broadcasted_iota(jnp.int32, (length, length), 0) >= lax.broadcasted_iota(
        jnp.int32, (length, length), 1
    )
    for pair in range(per // 2):
        outs, grads = [], []
        for h in (2 * pair, 2 * pair + 1):
            head = step * per + h
            at = slice(h * width, (h + 1) * width)
            x, dy = x_ref[:, at], dy_ref[:, at]
            col = column(cum, lanes, head)
            row = cumt_ref[h : h + 1, :]
            decay = jnp.exp(jnp.where(causal, col - row, -1e30))
            weights = scores_ref[...] * decay
            narrow = weights.astype(BF16)
            outs.append(dot(narrow, x, 1, 0))
            grads.append(dot(narrow, dy, 0, 0))
            dw = dot(dy, x, 1, 1).astype(BF16).astype(F32)
            dsc_ref[...] += dw * decay
            pull = dw * weights
            rows_ref[...] += jnp.where(lanes == head, jnp.sum(pull, axis=1, keepdims=True), 0.0)
            cols_ref[h : h + 1, :] = jnp.sum(pull, axis=0, keepdims=True)
        at = slice(pair * 2 * width, (pair + 1) * 2 * width)
        gain = gain_ref[:, at]
        y_ref[:, at] = jnp.concatenate(outs, axis=1) + gain * x_ref[:, at].astype(F32)
        dx_ref[:, at] = jnp.concatenate(grads, axis=1) + gain * dy_ref[:, at].astype(F32)


def carried_kernel(
    x_ref, dy_ref, y_ref, dx_ref, e_ref, l_ref, cum_ref, b_ref, c_ref, dsc_ref, net_ref,
    out_ref, grad_ref, db_ref, dc_ref, dla_ref, q_ref, r_ref, el_ref, *, per, width,
):
    step = pl.program_id(0)

    @pl.when(step == 0)
    def _():
        q_ref[...] = net_ref[...]
        r_ref[...] = jnp.zeros_like(r_ref)
        el_ref[...] = jnp.zeros_like(el_ref)
        high, low = split(dsc_ref[...])
        db_ref[...] = dot(high, c_ref[...], 0, 0) + dot(low, c_ref[...], 0, 0)
        dc_ref[...] = dot(high, b_ref[...], 1, 0) + dot(low, b_ref[...], 1, 0)

    cum = cum_ref[...]
    length = cum.shape[0]
    lanes = lax.broadcasted_iota(jnp.int32, cum.shape, 1)
    lane_row = lanes[0:1, :]
    half = lax.broadcasted_iota(jnp.int32, (length, 2 * width), 1) < width
    into, outof = b_ref[...], c_ref[...]
    add_b, add_c = jnp.zeros_like(db_ref), jnp.zeros_like(dc_ref)
    add_q, add_r, add_el = jnp.zeros_like(q_ref), jnp.zeros_like(r_ref), jnp.zeros_like(el_ref)
    for pair in range(per // 2):
        head = step * per + 2 * pair
        both = jnp.where(half, column(cum, lanes, head), column(cum, lanes, head + 1))
        total = both[length - 1 : length, :]
        grow, tail = jnp.exp(both), jnp.exp(total - both)
        at = slice(pair * 2 * width, (pair + 1) * 2 * width)
        x, dy = x_ref[:, at].astype(F32), dy_ref[:, at].astype(F32)
        entering, leaving = e_ref[at, :], l_ref[at, :]
        eh, el = split(entering)
        lh, ll = split(leaving)
        carried = (dot(outof, eh, 1, 1) + dot(outof, el, 1, 1)) * grow
        pulled = (dot(into, lh, 1, 1) + dot(into, ll, 1, 1)) * tail
        out_ref[:, at] = (y_ref[:, at] + carried).astype(BF16)
        grad_ref[:, at] = (dx_ref[:, at] + pulled).astype(BF16)
        zh, zl = split(dy * grow)
        add_c += dot(zh, eh, 1, 0) + dot(zl, eh, 1, 0) + dot(zh, el, 1, 0)
        uh, ul = split(x * tail)
        add_b += dot(uh, lh, 1, 0) + dot(ul, lh, 1, 0) + dot(uh, ll, 1, 0)
        q, r, prod = dy * carried, x * pulled, entering * leaving
        for h in (0, 1):
            mine = half if h == 0 else jnp.logical_not(half)
            mark = lanes == head + h
            add_q += jnp.where(mark, jnp.sum(jnp.where(mine, q, 0.0), axis=1, keepdims=True), 0.0)
            add_r += jnp.where(mark, jnp.sum(jnp.where(mine, r, 0.0), axis=1, keepdims=True), 0.0)
            part = jnp.sum(prod[h * width : (h + 1) * width, :], axis=0, keepdims=True)
            add_el += jnp.where(lane_row == head + h, jnp.sum(part, axis=1, keepdims=True), 0.0)
    db_ref[...] += add_b
    dc_ref[...] += add_c
    q_ref[...] += add_q
    r_ref[...] += add_r
    el_ref[...] += add_el

    @pl.when(step == pl.num_programs(0) - 1)
    def _():
        i = lax.broadcasted_iota(jnp.int32, (length, length), 0)
        j = lax.broadcasted_iota(jnp.int32, (length, length), 1)
        after, before = (j >= i).astype(BF16), (j < i).astype(BF16)
        qh, ql = split(q_ref[...])
        rh, rl = split(r_ref[...])
        dla_ref[...] = (
            dot(after, qh, 1, 0) + dot(after, ql, 1, 0) + dot(before, rh, 1, 0) + dot(before, rl, 1, 0)
            + jnp.exp(cum[length - 1 : length, :]) * el_ref[...]
        )


def exponents(value):
    peak = jnp.max(jnp.abs(value), axis=(-2, -1))
    return jnp.ceil(jnp.log2(jnp.maximum(peak, TINY)))


def lane_row(table, lanes):
    pad = [(0, 0)] * (table.ndim - 1) + [(0, lanes - table.shape[-1])]
    return jnp.pad(table, pad)[..., None, :]


def pack(value, extra=()):
    power = exponents(value)
    lanes = value.shape[-1]
    rows = (value * jnp.exp2(-power)[..., None, None]).astype(F16)
    rows = rows.reshape(*value.shape[:-3], -1, lanes)
    tail = jnp.concatenate([lane_row(t, lanes) for t in (power, *extra)], axis=-2).astype(F16)
    pad = [(0, 0)] * (tail.ndim - 2) + [(0, TAIL_ROWS - tail.shape[-2]), (0, 0)]
    return jnp.concatenate([rows, jnp.pad(tail, pad)], axis=-2)


def unpack(rows, heads):
    body, tail = rows[..., :-TAIL_ROWS, :], rows[..., -TAIL_ROWS:, :].astype(F32)
    body = body.reshape(*body.shape[:-2], heads, -1, body.shape[-1]).astype(F32)
    tail = tail[..., :heads]
    return body * jnp.exp2(tail[..., 0, :])[..., None, None], tail


def three(value):
    terms = []
    for _ in range(3):
        terms.append(lax.reduce_precision(value, 5, 10))
        value = value - terms[-1]
    return terms


def chain(total, log_total, axis, backward):
    count = lax.axis_size(axis)
    heads = total.shape[0]
    own, own_log = total, log_total
    entering, entering_log = jnp.zeros_like(total), jnp.zeros_like(log_total)
    reach = 1
    while reach < count:
        pairs = [(i, i + reach) for i in range(count - reach)]
        if backward:
            pairs = [(b, a) for a, b in pairs]
        sent = pack(own, three(own_log))
        got, tail = unpack(lax.ppermute(sent, axis, pairs), heads)
        got_log = tail[1] + tail[2] + tail[3]
        entering = entering + jnp.exp(entering_log)[:, None, None] * got
        own = own + jnp.exp(own_log)[:, None, None] * got
        entering_log, own_log = entering_log + got_log, own_log + got_log
        reach *= 2
    return entering


def shards(signal, cotangent, input_map, output_map, log_decay, skip_gain):
    members = lax.axis_size("head")
    member = lax.axis_index("head")
    length, channels = signal.shape
    own_heads = log_decay.shape[1]
    heads = own_heads * members
    width = channels // heads
    state = input_map.shape[1]
    per = STEP_HEADS
    steps = heads // per
    lane_block = per * width

    by_member = log_decay.reshape(members, length, own_heads)
    gain_rows = jnp.broadcast_to(skip_gain, (members, 8, own_heads))
    rates = lax.all_to_all(
        jnp.concatenate([by_member, gain_rows], axis=1), "head", split_axis=0, concat_axis=0, tiled=True
    )
    rates = jnp.swapaxes(rates, 0, 1).reshape(length + 8, heads)
    decay, gains = rates[:length], rates[length]
    into = lax.dynamic_slice_in_dim(input_map, member * length, length, 0)
    outof = lax.dynamic_slice_in_dim(output_map, member * length, length, 0)
    lower = (
        lax.broadcasted_iota(jnp.int32, (length, length), 0)
        >= lax.broadcasted_iota(jnp.int32, (length, length), 1)
    ).astype(F32)
    cum = jnp.dot(lower, decay, precision=lax.Precision.HIGHEST)
    cum_t = cum.T
    gain_row = jnp.repeat(gains, width)[None, :]

    wide = pl.BlockSpec((length, lane_block), lambda k: (0, k))
    tall = pl.BlockSpec((lane_block, state), lambda k: (k, 0))

    def whole(*shape):
        return pl.BlockSpec(shape, lambda k: (0, 0))

    def call(body, name, in_specs, out_specs, out_shape, scratch=(), flops=0):
        return pl.pallas_call(
            lambda *refs: body(*refs, per=per, width=width),
            grid=(steps,), in_specs=in_specs, out_specs=out_specs, out_shape=out_shape,
            scratch_shapes=scratch, name=name,
            cost_estimate=pl.CostEstimate(flops=flops, transcendentals=0, bytes_accessed=16 * length * channels),
        )

    sd = jax.ShapeDtypeStruct
    maps = [whole(length, state)] * 2
    own_state, own_seed = call(
        states_kernel, "states", [wide, wide, whole(length, heads)] + maps, [tall, tall],
        [sd((channels, state), F32)] * 2, flops=8 * length * channels * state,
    )(signal, cotangent, cum, into, outof)

    def swap(f, b):
        both = jnp.concatenate([pack(f), pack(b)], axis=-1)
        both = lax.all_to_all(both, "head", split_axis=0, concat_axis=0, tiled=True)
        return [unpack(half, own_heads)[0] for half in (both[..., :state], both[..., state:])]

    shape = (members, own_heads, width, state)
    parts_f, parts_b = swap(own_state.reshape(shape), own_seed.reshape(shape))

    y_local, dx_local, dscores, rows, cols = call(
        within_kernel, "within",
        [wide, wide, whole(length, heads), pl.BlockSpec((per, length), lambda k: (k, 0))] + maps
        + [pl.BlockSpec((1, lane_block), lambda k: (0, k))],
        [wide, wide, whole(length, length), whole(length, heads),
         pl.BlockSpec((per, length), lambda k: (k, 0))],
        [sd((length, channels), F32)] * 2
        + [sd((length, length), F32), sd((length, heads), F32), sd((heads, length), F32)],
        scratch=[pltpu.VMEM((length, length), F32)], flops=24 * length * length * channels,
    )(signal, cotangent, cum, cum_t, into, outof, gain_row)

    logs = jnp.sum(by_member, axis=1)
    keep = jnp.exp(logs)[:, :, None, None]
    group_f, group_b = parts_f[0], parts_b[-1]
    for s in range(1, members):
        group_f = keep[s] * group_f + parts_f[s]
        group_b = keep[members - 1 - s] * group_b + parts_b[members - 1 - s]
    group_log = jnp.sum(logs, axis=0)
    list_f = [chain(group_f, group_log, "ctx", False)]
    list_b = [chain(group_b, group_log, "ctx", True)]
    for s in range(members - 1):
        list_f.append(keep[s] * list_f[-1] + parts_f[s])
        list_b.append(keep[members - 1 - s] * list_b[-1] + parts_b[members - 1 - s])
    e_all, l_all = swap(jnp.stack(list_f), jnp.stack(list_b[::-1]))
    e_all, l_all = e_all.reshape(channels, state), l_all.reshape(channels, state)

    scan_out, grad_signal, grad_in, grad_out, grad_decay = call(
        carried_kernel, "carried",
        [wide, wide, wide, wide, tall, tall, whole(length, heads)] + maps
        + [whole(length, length), whole(length, heads)],
        [wide, wide, whole(length, state), whole(length, state), whole(length, heads)],
        [sd((length, channels), BF16)] * 2 + [sd((length, state), F32)] * 2 + [sd((length, heads), F32)],
        scratch=[pltpu.VMEM((length, heads), F32)] * 2 + [pltpu.VMEM((1, heads), F32)],
        flops=20 * length * channels * state,
    )(signal, cotangent, y_local, dx_local, e_all, l_all, cum, into, outof, dscores, rows - cols.T)

    maps_out = lax.all_gather(jnp.concatenate([grad_in, grad_out], axis=1), "head", tiled=True)
    grad_decay = lax.all_to_all(grad_decay, "head", split_axis=1, concat_axis=0, tiled=True)
    return (scan_out, grad_signal, maps_out[:, :state], maps_out[:, state:], grad_decay)


def solution(mesh):
    return jax.shard_map(
        shards,
        mesh=mesh,
        in_specs=(
            P(("ctx", "head"), None),
            P(("ctx", "head"), None),
            P("ctx", None),
            P("ctx", None),
            P("ctx", "head"),
            P("head"),
        ),
        out_specs=(
            P(("ctx", "head"), None),
            P(("ctx", "head"), None),
            P("ctx", None),
            P("ctx", None),
            P("ctx", "head"),
        ),
        check_vma=False,
    )
```

```python
import functools

import jax
import jax.numpy as jnp
from jax import lax
from jax.experimental import pallas as pl
from jax.experimental.pallas import tpu as pltpu
from jax.sharding import PartitionSpec as P

F32, BF16, F16 = jnp.float32, jnp.bfloat16, jnp.float16
TINY = 1e-30
STEP_HEADS = 8
STREAMS = 2


def split(value):
    high = value.astype(BF16)
    return high, (value - high.astype(F32)).astype(BF16)


def dot(a, b, ca, cb):
    return lax.dot_general(a, b, (((ca,), (cb,)), ((), ())), preferred_element_type=F32)


def column(table, lanes, head):
    return jnp.sum(jnp.where(lanes == head, table, 0.0), axis=1, keepdims=True)


def states_kernel(x_ref, dy_ref, cum_ref, b_ref, c_ref, s_ref, r_ref, *, per, width):
    step = pl.program_id(0)
    cum = cum_ref[...]
    length = cum.shape[0]
    lanes = lax.broadcasted_iota(jnp.int32, cum.shape, 1)
    half = lax.broadcasted_iota(jnp.int32, (length, 2 * width), 1) < width
    into, outof = b_ref[...], c_ref[...]
    for pair in range(per // 2):
        first = column(cum, lanes, step * per + 2 * pair)
        second = column(cum, lanes, step * per + 2 * pair + 1)
        both = jnp.where(half, first, second)
        total = both[length - 1 : length, :]
        at = slice(pair * 2 * width, (pair + 1) * 2 * width)
        xs = split(x_ref[:, at].astype(F32) * jnp.exp(total - both))
        ds = split(dy_ref[:, at].astype(F32) * jnp.exp(both))
        s_ref[at, :] = dot(xs[0], into, 0, 0) + dot(xs[1], into, 0, 0)
        r_ref[at, :] = dot(ds[0], outof, 0, 0) + dot(ds[1], outof, 0, 0)


def within_kernel(
    x_ref, dy_ref, cum_ref, cumt_ref, b_ref, c_ref, gain_ref, *rest, per, width, first,
):
    y_ref, dx_ref, dsc_ref, rows_ref, cols_ref, scores_ref = rest[-6:]
    step = pl.program_id(0) + first

    @pl.when(step == first)
    def _():
        scores_ref[...] = dot(c_ref[...], b_ref[...], 1, 1)
        dsc_ref[...] = jnp.zeros_like(dsc_ref)
        rows_ref[...] = jnp.zeros_like(rows_ref)

    cum = cum_ref[...]
    length = cum.shape[0]
    lanes = lax.broadcasted_iota(jnp.int32, cum.shape, 1)
    causal = lax.broadcasted_iota(jnp.int32, (length, length), 0) >= lax.broadcasted_iota(
        jnp.int32, (length, length), 1
    )
    for pair in range(per // 2):
        outs, grads = [], []
        for h in (2 * pair, 2 * pair + 1):
            head = step * per + h
            at = slice(h * width, (h + 1) * width)
            x, dy = x_ref[:, at], dy_ref[:, at]
            col = column(cum, lanes, head)
            row = cumt_ref[h : h + 1, :]
            decay = jnp.exp(jnp.where(causal, col - row, -1e30))
            weights = scores_ref[...] * decay
            narrow = weights.astype(BF16)
            outs.append(dot(narrow, x, 1, 0))
            grads.append(dot(narrow, dy, 0, 0))
            dw = dot(dy, x, 1, 1).astype(BF16).astype(F32)
            dsc_ref[...] += dw * decay
            pull = dw * weights
            rows_ref[...] += jnp.where(lanes == head, jnp.sum(pull, axis=1, keepdims=True), 0.0)
            cols_ref[h : h + 1, :] = jnp.sum(pull, axis=0, keepdims=True)
        at = slice(pair * 2 * width, (pair + 1) * 2 * width)
        gain = gain_ref[:, at]
        y_ref[:, at] = jnp.concatenate(outs, axis=1) + gain * x_ref[:, at].astype(F32)
        dx_ref[:, at] = jnp.concatenate(grads, axis=1) + gain * dy_ref[:, at].astype(F32)


def carried_kernel(
    x_ref, dy_ref, y_ref, dx_ref, e_ref, l_ref, cum_ref, b_ref, c_ref, dsc_ref, net_ref,
    out_ref, grad_ref, db_ref, dc_ref, dla_ref, q_ref, r_ref, el_ref, *, per, width,
):
    step = pl.program_id(0)

    @pl.when(step == 0)
    def _():
        q_ref[...] = net_ref[...]
        r_ref[...] = jnp.zeros_like(r_ref)
        el_ref[...] = jnp.zeros_like(el_ref)
        high, low = split(dsc_ref[...])
        db_ref[...] = dot(high, c_ref[...], 0, 0) + dot(low, c_ref[...], 0, 0)
        dc_ref[...] = dot(high, b_ref[...], 1, 0) + dot(low, b_ref[...], 1, 0)

    cum = cum_ref[...]
    length = cum.shape[0]
    lanes = lax.broadcasted_iota(jnp.int32, cum.shape, 1)
    lane_row = lanes[0:1, :]
    half = lax.broadcasted_iota(jnp.int32, (length, 2 * width), 1) < width
    into, outof = b_ref[...], c_ref[...]
    add_b, add_c = jnp.zeros_like(db_ref), jnp.zeros_like(dc_ref)
    add_q, add_r, add_el = jnp.zeros_like(q_ref), jnp.zeros_like(r_ref), jnp.zeros_like(el_ref)
    for pair in range(per // 2):
        head = step * per + 2 * pair
        both = jnp.where(half, column(cum, lanes, head), column(cum, lanes, head + 1))
        total = both[length - 1 : length, :]
        grow, tail = jnp.exp(both), jnp.exp(total - both)
        at = slice(pair * 2 * width, (pair + 1) * 2 * width)
        x, dy = x_ref[:, at].astype(F32), dy_ref[:, at].astype(F32)
        entering, leaving = e_ref[at, :], l_ref[at, :]
        eh, el = split(entering)
        lh, ll = split(leaving)
        carried = (dot(outof, eh, 1, 1) + dot(outof, el, 1, 1)) * grow
        pulled = (dot(into, lh, 1, 1) + dot(into, ll, 1, 1)) * tail
        out_ref[:, at] = (y_ref[:, at] + carried).astype(BF16)
        grad_ref[:, at] = (dx_ref[:, at] + pulled).astype(BF16)
        zh, zl = split(dy * grow)
        add_c += dot(zh, eh, 1, 0) + dot(zl, eh, 1, 0) + dot(zh, el, 1, 0)
        uh, ul = split(x * tail)
        add_b += dot(uh, lh, 1, 0) + dot(ul, lh, 1, 0) + dot(uh, ll, 1, 0)
        q, r, prod = dy * carried, x * pulled, entering * leaving
        for h in (0, 1):
            mine = half if h == 0 else jnp.logical_not(half)
            mark = lanes == head + h
            add_q += jnp.where(mark, jnp.sum(jnp.where(mine, q, 0.0), axis=1, keepdims=True), 0.0)
            add_r += jnp.where(mark, jnp.sum(jnp.where(mine, r, 0.0), axis=1, keepdims=True), 0.0)
            part = jnp.sum(prod[h * width : (h + 1) * width, :], axis=0, keepdims=True)
            add_el += jnp.where(lane_row == head + h, jnp.sum(part, axis=1, keepdims=True), 0.0)
    db_ref[...] += add_b
    dc_ref[...] += add_c
    q_ref[...] += add_q
    r_ref[...] += add_r
    el_ref[...] += add_el

    @pl.when(step == pl.num_programs(0) - 1)
    def _():
        i = lax.broadcasted_iota(jnp.int32, (length, length), 0)
        j = lax.broadcasted_iota(jnp.int32, (length, length), 1)
        after, before = (j >= i).astype(BF16), (j < i).astype(BF16)
        qh, ql = split(q_ref[...])
        rh, rl = split(r_ref[...])
        dla_ref[...] = (
            dot(after, qh, 1, 0) + dot(after, ql, 1, 0) + dot(before, rh, 1, 0) + dot(before, rl, 1, 0)
            + jnp.exp(cum[length - 1 : length, :]) * el_ref[...]
        )


def chain(total, logs, axis, backward):
    count, mine = logs.shape[0], lax.axis_index(axis)
    own, entering = total, None
    own_log, entering_log = logs, jnp.zeros_like(logs)
    reach = 1
    while reach < count:
        pairs = [(i, i + reach) for i in range(count - reach)]
        if backward:
            pairs = [(b, a) for a, b in pairs]
        got = lax.ppermute(own.astype(F16), axis, pairs).astype(F32)

        def factor(table):
            row = lax.dynamic_index_in_dim(table, mine, 0, keepdims=False)
            return jnp.exp(row)[:, None, None]

        scaled = factor(entering_log) * got
        entering = scaled if entering is None else entering + scaled
        own = own + factor(own_log) * got
        blank = jnp.zeros_like(logs[:reach])
        if backward:
            moved = jnp.concatenate([own_log[reach:], blank], axis=0)
        else:
            moved = jnp.concatenate([blank, own_log[:-reach]], axis=0)
        entering_log, own_log = entering_log + moved, own_log + moved
        reach *= 2
    return entering


def largest(value):
    return jnp.max(jnp.abs(value)).astype(F32)


def shards(signal, cotangent, input_map, output_map, log_decay, skip_gain):
    members, blocks = lax.axis_size("head"), lax.axis_size("ctx")
    member = lax.axis_index("head")
    length, channels = signal.shape
    own_heads = log_decay.shape[1]
    heads = own_heads * members
    width = channels // heads
    state = input_map.shape[1]
    per = STEP_HEADS
    steps = heads // per
    lane_block = per * width

    by_member = log_decay.reshape(members, length, own_heads)
    peaks = jnp.stack([largest(signal), largest(cotangent)])
    known = jnp.zeros((8, own_heads), F32).at[0].set(skip_gain).at[1:3].set(peaks[:, None])
    rates = lax.all_to_all(
        jnp.concatenate([by_member, jnp.broadcast_to(known, (members, 8, own_heads))], axis=1),
        "head", split_axis=0, concat_axis=0, tiled=True,
    )
    logs = jnp.sum(by_member, axis=1)
    maps_peak = jnp.stack([largest(input_map), largest(output_map)])
    bounds = jnp.max(rates[:, length + 1 : length + 3, 0], axis=0) * maps_peak
    told = jnp.stack([jnp.sum(logs, axis=0), *jnp.broadcast_to(bounds[:, None], (2, own_heads))])
    told = lax.all_to_all(
        jnp.broadcast_to(told, (blocks, 3, own_heads)), "ctx", split_axis=0, concat_axis=0, tiled=True
    )
    block_logs = told[:, 0]
    terms = blocks * members * length
    limits = jnp.maximum(jnp.max(told[:, 1:, 0], axis=0) * terms, TINY)
    grow = jnp.exp2(14.0 - jnp.ceil(jnp.log2(limits)))
    rates = jnp.swapaxes(rates, 0, 1).reshape(length + 8, heads)
    decay, gains = rates[:length], rates[length]
    into = lax.dynamic_slice_in_dim(input_map, member * length, length, 0)
    outof = lax.dynamic_slice_in_dim(output_map, member * length, length, 0)
    lower = (
        lax.broadcasted_iota(jnp.int32, (length, length), 0)
        >= lax.broadcasted_iota(jnp.int32, (length, length), 1)
    ).astype(F32)
    cum = jnp.dot(lower, decay, precision=lax.Precision.HIGHEST)
    cum_t = cum.T
    gain_row = jnp.repeat(gains, width)[None, :]

    wide = pl.BlockSpec((length, lane_block), lambda k: (0, k))
    tall = pl.BlockSpec((lane_block, state), lambda k: (k, 0))

    def whole(*shape):
        return pl.BlockSpec(shape, lambda k: (0, 0))

    def call(body, name, in_specs, out_specs, out_shape, scratch=(), flops=0):
        return pl.pallas_call(
            lambda *refs: body(*refs, per=per, width=width),
            grid=(steps,), in_specs=in_specs, out_specs=out_specs, out_shape=out_shape,
            scratch_shapes=scratch, name=name,
            cost_estimate=pl.CostEstimate(flops=flops, transcendentals=0, bytes_accessed=16 * length * channels),
        )

    sd = jax.ShapeDtypeStruct
    maps = [whole(length, state)] * 2
    own_state, own_seed = call(
        states_kernel, "states", [wide, wide, whole(length, heads)] + maps, [tall, tall],
        [sd((channels, state), F32)] * 2, flops=8 * length * channels * state,
    )(signal, cotangent, cum, into, outof)

    shape = (members, own_heads, width, state)
    piece = own_heads // STREAMS
    pieces = [slice(i * piece, (i + 1) * piece) for i in range(STREAMS)]

    def swap(f, b):
        both = jnp.concatenate([f.astype(F16), b.astype(F16)], axis=-1)
        both = both.reshape(members, piece * width, 2 * state)
        both = lax.all_to_all(both, "head", split_axis=0, concat_axis=0, tiled=True)
        both = both.reshape(members, piece, width, 2 * state)
        return both[..., :state], both[..., state:]

    sums_f, sums_b = own_state.reshape(shape), own_seed.reshape(shape)
    arrived = [swap(sums_f[:, at] * grow[0], sums_b[:, at] * grow[1]) for at in pieces]

    def within(first, last, earlier):
        wide_at = pl.BlockSpec((length, lane_block), lambda k: (0, k + first))
        rows_at = pl.BlockSpec((per, length), lambda k: (k + first, 0))
        gain_at = pl.BlockSpec((1, lane_block), lambda k: (0, k + first))
        return pl.pallas_call(
            functools.partial(within_kernel, per=per, width=width, first=first),
            grid=(last - first,),
            in_specs=[wide_at, wide_at, whole(length, heads), rows_at] + maps + [gain_at]
            + [pl.BlockSpec(memory_space=pl.ANY)] * len(earlier),
            out_specs=[wide_at, wide_at, whole(length, length), whole(length, heads), rows_at],
            out_shape=[sd((length, channels), F32)] * 2
            + [sd((length, length), F32), sd((length, heads), F32), sd((heads, length), F32)],
            scratch_shapes=[pltpu.VMEM((length, length), F32)], name="within",
            input_output_aliases=dict(zip((7, 8, 9), (0, 1, 4))) if earlier else {},
            cost_estimate=pl.CostEstimate(
                flops=24 * length * length * channels, transcendentals=0,
                bytes_accessed=16 * length * channels,
            ),
        )(signal, cotangent, cum, cum_t, into, outof, gain_row, *earlier)

    y_half, dx_half, dscores_a, rows_a, cols_half = within(0, steps // 2, ())
    arrived[0], rows_a = lax.optimization_barrier((arrived[0], rows_a))

    homes, ready = [], None
    for at, (parts_f, parts_b) in zip(pieces, arrived):
        if ready is not None:
            parts_f, parts_b, ready = lax.optimization_barrier((parts_f, parts_b, ready))
        parts_f, parts_b = parts_f.astype(F32), parts_b.astype(F32)
        keep = jnp.exp(logs[:, at])[:, :, None, None]
        group_f, group_b = parts_f[0], parts_b[-1]
        for s in range(1, members):
            group_f = keep[s] * group_f + parts_f[s]
            group_b = keep[members - 1 - s] * group_b + parts_b[members - 1 - s]
        list_f = [chain(group_f, block_logs[:, at], "ctx", False)]
        list_b = [chain(group_b, block_logs[:, at], "ctx", True)]
        ready = list_f[0][0, :8] + list_b[0][0, :8]
        for s in range(members - 1):
            list_f.append(keep[s] * list_f[-1] + parts_f[s])
            list_b.append(keep[members - 1 - s] * list_b[-1] + parts_b[members - 1 - s])
        homes.append(swap(jnp.stack(list_f), jnp.stack(list_b[::-1])))
    y_local, dx_local, dscores_b, rows_b, cols = within(steps // 2, steps, (y_half, dx_half, cols_half))
    dscores, rows = dscores_a + dscores_b, rows_a + rows_b
    e_all = jnp.concatenate([h[0] for h in homes], axis=1).astype(F32) / grow[0]
    l_all = jnp.concatenate([h[1] for h in homes], axis=1).astype(F32) / grow[1]
    e_all, l_all = e_all.reshape(channels, state), l_all.reshape(channels, state)

    scan_out, grad_signal, grad_in, grad_out, grad_decay = call(
        carried_kernel, "carried",
        [wide, wide, wide, wide, tall, tall, whole(length, heads)] + maps
        + [whole(length, length), whole(length, heads)],
        [wide, wide, whole(length, state), whole(length, state), whole(length, heads)],
        [sd((length, channels), BF16)] * 2 + [sd((length, state), F32)] * 2 + [sd((length, heads), F32)],
        scratch=[pltpu.VMEM((length, heads), F32)] * 2 + [pltpu.VMEM((1, heads), F32)],
        flops=20 * length * channels * state,
    )(signal, cotangent, y_local, dx_local, e_all, l_all, cum, into, outof, dscores, rows - cols.T)

    maps_out = lax.all_gather(jnp.concatenate([grad_in, grad_out], axis=1), "head", tiled=True)
    grad_decay = lax.all_to_all(grad_decay, "head", split_axis=1, concat_axis=0, tiled=True)
    return (scan_out, grad_signal, maps_out[:, :state], maps_out[:, state:], grad_decay)


def solution(mesh):
    return jax.shard_map(
        shards,
        mesh=mesh,
        in_specs=(
            P(("ctx", "head"), None),
            P(("ctx", "head"), None),
            P("ctx", None),
            P("ctx", None),
            P("ctx", "head"),
            P("head"),
        ),
        out_specs=(
            P(("ctx", "head"), None),
            P(("ctx", "head"), None),
            P("ctx", None),
            P("ctx", None),
            P("ctx", "head"),
        ),
        check_vma=False,
    )
```

```python
import jax
import jax.numpy as jnp
from jax import lax
from jax.experimental import pallas as pl
from jax.experimental.pallas import tpu as pltpu
from jax.sharding import PartitionSpec as P

F32, BF16, F16 = jnp.float32, jnp.bfloat16, jnp.float16
TINY = 1e-30
STEP_HEADS = 8
STREAMS = 1


def split(value):
    high = value.astype(BF16)
    return high, (value - high.astype(F32)).astype(BF16)


def dot(a, b, ca, cb):
    return lax.dot_general(a, b, (((ca,), (cb,)), ((), ())), preferred_element_type=F32)


def column(table, lanes, head):
    return jnp.sum(jnp.where(lanes == head, table, 0.0), axis=1, keepdims=True)


def states_kernel(x_ref, dy_ref, cum_ref, b_ref, c_ref, s_ref, r_ref, *, per, width):
    step = pl.program_id(0)
    cum = cum_ref[...]
    length = cum.shape[0]
    lanes = lax.broadcasted_iota(jnp.int32, cum.shape, 1)
    half = lax.broadcasted_iota(jnp.int32, (length, 2 * width), 1) < width
    into, outof = b_ref[...], c_ref[...]
    for pair in range(per // 2):
        first = column(cum, lanes, step * per + 2 * pair)
        second = column(cum, lanes, step * per + 2 * pair + 1)
        both = jnp.where(half, first, second)
        total = both[length - 1 : length, :]
        at = slice(pair * 2 * width, (pair + 1) * 2 * width)
        xs = split(x_ref[:, at].astype(F32) * jnp.exp(total - both))
        ds = split(dy_ref[:, at].astype(F32) * jnp.exp(both))
        s_ref[at, :] = dot(xs[0], into, 0, 0) + dot(xs[1], into, 0, 0)
        r_ref[at, :] = dot(ds[0], outof, 0, 0) + dot(ds[1], outof, 0, 0)


def within_kernel(
    x_ref, dy_ref, cum_ref, cumt_ref, b_ref, c_ref, gain_ref,
    y_ref, dx_ref, dsc_ref, rows_ref, cols_ref, scores_ref, *, per, width,
):
    step = pl.program_id(0)

    @pl.when(step == 0)
    def _():
        scores_ref[...] = dot(c_ref[...], b_ref[...], 1, 1)
        dsc_ref[...] = jnp.zeros_like(dsc_ref)
        rows_ref[...] = jnp.zeros_like(rows_ref)

    cum = cum_ref[...]
    length = cum.shape[0]
    lanes = lax.broadcasted_iota(jnp.int32, cum.shape, 1)
    causal = lax.broadcasted_iota(jnp.int32, (length, length), 0) >= lax.broadcasted_iota(
        jnp.int32, (length, length), 1
    )
    for pair in range(per // 2):
        outs, grads = [], []
        for h in (2 * pair, 2 * pair + 1):
            head = step * per + h
            at = slice(h * width, (h + 1) * width)
            x, dy = x_ref[:, at], dy_ref[:, at]
            col = column(cum, lanes, head)
            row = cumt_ref[h : h + 1, :]
            decay = jnp.exp(jnp.where(causal, col - row, -1e30))
            weights = scores_ref[...] * decay
            narrow = weights.astype(BF16)
            outs.append(dot(narrow, x, 1, 0))
            grads.append(dot(narrow, dy, 0, 0))
            dw = dot(dy, x, 1, 1).astype(BF16).astype(F32)
            dsc_ref[...] += dw * decay
            pull = dw * weights
            rows_ref[...] += jnp.where(lanes == head, jnp.sum(pull, axis=1, keepdims=True), 0.0)
            cols_ref[h : h + 1, :] = jnp.sum(pull, axis=0, keepdims=True)
        at = slice(pair * 2 * width, (pair + 1) * 2 * width)
        gain = gain_ref[:, at]
        y_ref[:, at] = jnp.concatenate(outs, axis=1) + gain * x_ref[:, at].astype(F32)
        dx_ref[:, at] = jnp.concatenate(grads, axis=1) + gain * dy_ref[:, at].astype(F32)


def carried_kernel(
    x_ref, dy_ref, y_ref, dx_ref, e_ref, l_ref, cum_ref, b_ref, c_ref, dsc_ref, net_ref,
    out_ref, grad_ref, db_ref, dc_ref, dla_ref, q_ref, r_ref, el_ref, *, per, width,
):
    step = pl.program_id(0)

    @pl.when(step == 0)
    def _():
        q_ref[...] = net_ref[...]
        r_ref[...] = jnp.zeros_like(r_ref)
        el_ref[...] = jnp.zeros_like(el_ref)
        high, low = split(dsc_ref[...])
        db_ref[...] = dot(high, c_ref[...], 0, 0) + dot(low, c_ref[...], 0, 0)
        dc_ref[...] = dot(high, b_ref[...], 1, 0) + dot(low, b_ref[...], 1, 0)

    cum = cum_ref[...]
    length = cum.shape[0]
    lanes = lax.broadcasted_iota(jnp.int32, cum.shape, 1)
    lane_row = lanes[0:1, :]
    half = lax.broadcasted_iota(jnp.int32, (length, 2 * width), 1) < width
    into, outof = b_ref[...], c_ref[...]
    add_b, add_c = jnp.zeros_like(db_ref), jnp.zeros_like(dc_ref)
    add_q, add_r, add_el = jnp.zeros_like(q_ref), jnp.zeros_like(r_ref), jnp.zeros_like(el_ref)
    for pair in range(per // 2):
        head = step * per + 2 * pair
        both = jnp.where(half, column(cum, lanes, head), column(cum, lanes, head + 1))
        total = both[length - 1 : length, :]
        grow, tail = jnp.exp(both), jnp.exp(total - both)
        at = slice(pair * 2 * width, (pair + 1) * 2 * width)
        x, dy = x_ref[:, at].astype(F32), dy_ref[:, at].astype(F32)
        entering, leaving = e_ref[at, :], l_ref[at, :]
        eh, el = split(entering)
        lh, ll = split(leaving)
        carried = (dot(outof, eh, 1, 1) + dot(outof, el, 1, 1)) * grow
        pulled = (dot(into, lh, 1, 1) + dot(into, ll, 1, 1)) * tail
        out_ref[:, at] = (y_ref[:, at] + carried).astype(BF16)
        grad_ref[:, at] = (dx_ref[:, at] + pulled).astype(BF16)
        zh, zl = split(dy * grow)
        add_c += dot(zh, eh, 1, 0) + dot(zl, eh, 1, 0) + dot(zh, el, 1, 0)
        uh, ul = split(x * tail)
        add_b += dot(uh, lh, 1, 0) + dot(ul, lh, 1, 0) + dot(uh, ll, 1, 0)
        q, r, prod = dy * carried, x * pulled, entering * leaving
        for h in (0, 1):
            mine = half if h == 0 else jnp.logical_not(half)
            mark = lanes == head + h
            add_q += jnp.where(mark, jnp.sum(jnp.where(mine, q, 0.0), axis=1, keepdims=True), 0.0)
            add_r += jnp.where(mark, jnp.sum(jnp.where(mine, r, 0.0), axis=1, keepdims=True), 0.0)
            part = jnp.sum(prod[h * width : (h + 1) * width, :], axis=0, keepdims=True)
            add_el += jnp.where(lane_row == head + h, jnp.sum(part, axis=1, keepdims=True), 0.0)
    db_ref[...] += add_b
    dc_ref[...] += add_c
    q_ref[...] += add_q
    r_ref[...] += add_r
    el_ref[...] += add_el

    @pl.when(step == pl.num_programs(0) - 1)
    def _():
        i = lax.broadcasted_iota(jnp.int32, (length, length), 0)
        j = lax.broadcasted_iota(jnp.int32, (length, length), 1)
        after, before = (j >= i).astype(BF16), (j < i).astype(BF16)
        qh, ql = split(q_ref[...])
        rh, rl = split(r_ref[...])
        dla_ref[...] = (
            dot(after, qh, 1, 0) + dot(after, ql, 1, 0) + dot(before, rh, 1, 0) + dot(before, rl, 1, 0)
            + jnp.exp(cum[length - 1 : length, :]) * el_ref[...]
        )


def chain(total, logs, axis, backward):
    count, mine = logs.shape[0], lax.axis_index(axis)
    own, entering = total, None
    own_log, entering_log = logs, jnp.zeros_like(logs)
    reach = 1
    while reach < count:
        pairs = [(i, i + reach) for i in range(count - reach)]
        if backward:
            pairs = [(b, a) for a, b in pairs]
        got = lax.ppermute(own.astype(F16), axis, pairs).astype(F32)

        def factor(table):
            row = lax.dynamic_index_in_dim(table, mine, 0, keepdims=False)
            return jnp.exp(row)[:, None, None]

        scaled = factor(entering_log) * got
        entering = scaled if entering is None else entering + scaled
        own = own + factor(own_log) * got
        blank = jnp.zeros_like(logs[:reach])
        if backward:
            moved = jnp.concatenate([own_log[reach:], blank], axis=0)
        else:
            moved = jnp.concatenate([blank, own_log[:-reach]], axis=0)
        entering_log, own_log = entering_log + moved, own_log + moved
        reach *= 2
    return entering


def largest(value):
    return jnp.max(jnp.abs(value)).astype(F32)


def shards(signal, cotangent, input_map, output_map, log_decay, skip_gain):
    members, blocks = lax.axis_size("head"), lax.axis_size("ctx")
    member = lax.axis_index("head")
    length, channels = signal.shape
    own_heads = log_decay.shape[1]
    heads = own_heads * members
    width = channels // heads
    state = input_map.shape[1]
    per = STEP_HEADS
    steps = heads // per
    lane_block = per * width

    by_member = log_decay.reshape(members, length, own_heads)
    peaks = jnp.stack([largest(signal), largest(cotangent)])
    known = jnp.zeros((8, own_heads), F32).at[0].set(skip_gain).at[1:3].set(peaks[:, None])
    rates = lax.all_to_all(
        jnp.concatenate([by_member, jnp.broadcast_to(known, (members, 8, own_heads))], axis=1),
        "head", split_axis=0, concat_axis=0, tiled=True,
    )
    logs = jnp.sum(by_member, axis=1)
    maps_peak = jnp.stack([largest(input_map), largest(output_map)])
    bounds = jnp.max(rates[:, length + 1 : length + 3, 0], axis=0) * maps_peak
    told = jnp.stack([jnp.sum(logs, axis=0), *jnp.broadcast_to(bounds[:, None], (2, own_heads))])
    told = lax.all_to_all(
        jnp.broadcast_to(told, (blocks, 3, own_heads)), "ctx", split_axis=0, concat_axis=0, tiled=True
    )
    block_logs = told[:, 0]
    terms = blocks * members * length
    limits = jnp.maximum(jnp.max(told[:, 1:, 0], axis=0) * terms, TINY)
    grow = jnp.exp2(14.0 - jnp.ceil(jnp.log2(limits)))
    rates = jnp.swapaxes(rates, 0, 1).reshape(length + 8, heads)
    decay, gains = rates[:length], rates[length]
    into = lax.dynamic_slice_in_dim(input_map, member * length, length, 0)
    outof = lax.dynamic_slice_in_dim(output_map, member * length, length, 0)
    lower = (
        lax.broadcasted_iota(jnp.int32, (length, length), 0)
        >= lax.broadcasted_iota(jnp.int32, (length, length), 1)
    ).astype(F32)
    cum = jnp.dot(lower, decay, precision=lax.Precision.HIGHEST)
    cum_t = cum.T
    gain_row = jnp.repeat(gains, width)[None, :]

    wide = pl.BlockSpec((length, lane_block), lambda k: (0, k))
    tall = pl.BlockSpec((lane_block, state), lambda k: (k, 0))

    def whole(*shape):
        return pl.BlockSpec(shape, lambda k: (0, 0))

    def call(body, name, in_specs, out_specs, out_shape, scratch=(), flops=0):
        return pl.pallas_call(
            lambda *refs: body(*refs, per=per, width=width),
            grid=(steps,), in_specs=in_specs, out_specs=out_specs, out_shape=out_shape,
            scratch_shapes=scratch, name=name,
            cost_estimate=pl.CostEstimate(flops=flops, transcendentals=0, bytes_accessed=16 * length * channels),
        )

    sd = jax.ShapeDtypeStruct
    maps = [whole(length, state)] * 2
    own_state, own_seed = call(
        states_kernel, "states", [wide, wide, whole(length, heads)] + maps, [tall, tall],
        [sd((channels, state), F32)] * 2, flops=8 * length * channels * state,
    )(signal, cotangent, cum, into, outof)

    shape = (members, own_heads, width, state)
    piece = own_heads // STREAMS
    pieces = [slice(i * piece, (i + 1) * piece) for i in range(STREAMS)]

    def swap(f, b):
        both = jnp.concatenate([f.astype(F16), b.astype(F16)], axis=-1)
        both = both.reshape(members, piece * width, 2 * state)
        both = lax.all_to_all(both, "head", split_axis=0, concat_axis=0, tiled=True)
        both = both.reshape(members, piece, width, 2 * state)
        return both[..., :state], both[..., state:]

    sums_f, sums_b = own_state.reshape(shape), own_seed.reshape(shape)
    arrived = [swap(sums_f[:, at] * grow[0], sums_b[:, at] * grow[1]) for at in pieces]

    y_local, dx_local, dscores, rows, cols = call(
        within_kernel, "within",
        [wide, wide, whole(length, heads), pl.BlockSpec((per, length), lambda k: (k, 0))] + maps
        + [pl.BlockSpec((1, lane_block), lambda k: (0, k))],
        [wide, wide, whole(length, length), whole(length, heads),
         pl.BlockSpec((per, length), lambda k: (k, 0))],
        [sd((length, channels), F32)] * 2
        + [sd((length, length), F32), sd((length, heads), F32), sd((heads, length), F32)],
        scratch=[pltpu.VMEM((length, length), F32)], flops=24 * length * length * channels,
    )(signal, cotangent, cum, cum_t, into, outof, gain_row)

    homes = []
    for at, (parts_f, parts_b) in zip(pieces, arrived):
        parts_f, parts_b = parts_f.astype(F32), parts_b.astype(F32)
        keep = jnp.exp(logs[:, at])[:, :, None, None]
        group_f, group_b = parts_f[0], parts_b[-1]
        for s in range(1, members):
            group_f = keep[s] * group_f + parts_f[s]
            group_b = keep[members - 1 - s] * group_b + parts_b[members - 1 - s]
        list_f = [chain(group_f, block_logs[:, at], "ctx", False)]
        list_b = [chain(group_b, block_logs[:, at], "ctx", True)]
        for s in range(members - 1):
            list_f.append(keep[s] * list_f[-1] + parts_f[s])
            list_b.append(keep[members - 1 - s] * list_b[-1] + parts_b[members - 1 - s])
        homes.append(swap(jnp.stack(list_f), jnp.stack(list_b[::-1])))
    e_all = jnp.concatenate([h[0] for h in homes], axis=1).astype(F32) / grow[0]
    l_all = jnp.concatenate([h[1] for h in homes], axis=1).astype(F32) / grow[1]
    e_all, l_all = e_all.reshape(channels, state), l_all.reshape(channels, state)

    scan_out, grad_signal, grad_in, grad_out, grad_decay = call(
        carried_kernel, "carried",
        [wide, wide, wide, wide, tall, tall, whole(length, heads)] + maps
        + [whole(length, length), whole(length, heads)],
        [wide, wide, whole(length, state), whole(length, state), whole(length, heads)],
        [sd((length, channels), BF16)] * 2 + [sd((length, state), F32)] * 2 + [sd((length, heads), F32)],
        scratch=[pltpu.VMEM((length, heads), F32)] * 2 + [pltpu.VMEM((1, heads), F32)],
        flops=20 * length * channels * state,
    )(signal, cotangent, y_local, dx_local, e_all, l_all, cum, into, outof, dscores, rows - cols.T)

    maps_out = lax.all_gather(jnp.concatenate([grad_in, grad_out], axis=1), "head", tiled=True)
    grad_decay = lax.all_to_all(grad_decay, "head", split_axis=1, concat_axis=0, tiled=True)
    return (scan_out, grad_signal, maps_out[:, :state], maps_out[:, state:], grad_decay)


def solution(mesh):
    return jax.shard_map(
        shards,
        mesh=mesh,
        in_specs=(
            P(("ctx", "head"), None),
            P(("ctx", "head"), None),
            P("ctx", None),
            P("ctx", None),
            P("ctx", "head"),
            P("head"),
        ),
        out_specs=(
            P(("ctx", "head"), None),
            P(("ctx", "head"), None),
            P("ctx", None),
            P("ctx", None),
            P("ctx", "head"),
        ),
        check_vma=False,
    )
```
